128 devices in a mesh: row: 8 (over z, y_hi), col: 16 (over x, y_lo, core).
Axes of the slice: x: 4, y: 4 (y_hi: 2, y_lo: 2; y = y_hi * 2 + y_lo), z: 4, core: 2. Of those that a mesh axis runs over, the one named last changes fastest.
Arguments:
- tokens: bfloat16 [1024, 8192], P('row', 'col'), may hold values from -6 to 6
- weight_in: bfloat16 [8192, 32768], P('col', 'row'), may hold values from -0.0625 to 0.0625
- weight_out: bfloat16 [32768, 8192], P('row', 'col'), may hold values from -0.03125 to 0.03125
- upstream: bfloat16 [1024, 8192], P('row', 'col'), may hold values from -1.5 to 1.5
Outputs:
- output: bfloat16 [1024, 8192], P('row', 'col')
- grad_tokens: bfloat16 [1024, 8192], P('row', 'col')
- grad_weight_in: bfloat16 [8192, 32768], P('col', 'row')
- grad_weight_out: bfloat16 [32768, 8192], P('row', 'col')
The draws below stay inside these ranges and needn't reach their ends.
All inputs are finite; a program needn't handle non-finite values.
Results may differ from the reference program's by a relative error of at most 0.0049.
Values may be sent and summed in bfloat16 or wider, within the bound.
No kernel may reach another device: no remote copies, remote signals or barrier semaphores. Data moves between devices by JAX's collectives and lax.ppermute only.
A program may use at most 128 MiB of HBM per device.

```python
import math
import jax
import jax.numpy as jnp
from jax import lax

D = 8192
FF = 32768
TOKENS = 1024


def raised(values, key, source, target, blocks, factor):
    owner, partner = [(jnp.arange(values.shape[axis_at]) // (values.shape[axis_at] // blocks)).reshape([-1 if axis == axis_at else 1 for axis in range(values.ndim)]) for axis_at in (source, target)]
    chosen = jax.random.permutation(key, blocks)[partner]
    strong = (owner == chosen) | (owner == (partner + blocks // 2) % blocks)
    return jnp.where(strong, factor * values, values)


def level_of(rng, extent, cuts, low, top_value):
    gain, own = 1.0, jax.random.fold_in(rng, 6)
    for position, blocks in cuts:
        steps = jnp.exp(jax.random.uniform(jax.random.fold_in(own, position), (blocks,), jnp.float32, low / len(cuts), top_value / len(cuts)))
        gain = gain * jnp.repeat(steps, extent[position] // blocks).reshape([-1 if axis == position else 1 for axis in range(len(extent))])
    return gain


def scatter_about(own_key, dims, width, most, cuts=(), kind=jnp.bfloat16):
    result = jax.random.normal(own_key, dims, jnp.float32) * width
    if len(cuts) > 0:
        result = level_of(own_key, dims, cuts, -0.22, 0.18) * result
    return jnp.clip(result, min=-most, max=most).astype(kind)


def bell_draw_with(stream_key, dims, scale, limit, split, heavy, dtype=jnp.bfloat16):
    array = scale * jax.random.normal(stream_key, dims, jnp.float32)
    if split:
        array = array * level_of(stream_key, dims, split, -0.22, 0.18)
    return jnp.clip(raised(array, jax.random.fold_in(stream_key, 3), *heavy), -limit, limit).astype(dtype)


def setup_inputs(seed: int = 0) -> dict:
    arg_keys = jax.random.split(jax.random.key(seed), 5)
    return {
        "tokens": bell_draw_with(arg_keys[0], (TOKENS, D), 1.0, 6.0, ((0, 8), (1, 16)), (1, 0, 16, 2.0)),
        "weight_in": scatter_about(arg_keys[1], (D, FF), D ** -0.5, 0.0625, ((0, 16), (1, 8))),
        "weight_out": scatter_about(arg_keys[2], (FF, D), FF ** -0.5, 0.03125, ((0, 8), (1, 16))),
        "upstream": bell_draw_with(arg_keys[3], (TOKENS, D), 0.25, 1.5, ((0, 8), (1, 16)), (1, 0, 16, 2.0)),
    }


def gelu_value(value):
    return 0.5 * value * (1.0 + jax.scipy.special.erf(value / math.sqrt(2.0)))

def gelu_slope(value):
    normal_part = jnp.exp(-0.5 * value * value) / math.sqrt(2.0 * math.pi)
    return 0.5 * (1.0 + jax.scipy.special.erf(value / math.sqrt(2.0))) + value * normal_part

def reference(tokens, weight_in, weight_out, upstream):
    hidden = jnp.dot(tokens, weight_in, preferred_element_type=jnp.float32)
    act = gelu_value(hidden).astype(jnp.bfloat16)
    output = jnp.dot(act, weight_out, preferred_element_type=jnp.float32).astype(jnp.bfloat16)
    grad_act = lax.dot_general(upstream, weight_out, (((1,), (1,)), ((), ())), preferred_element_type=jnp.float32)
    grad_hidden = (grad_act * gelu_slope(hidden)).astype(jnp.bfloat16)
    grad_weight_out = lax.dot_general(act, upstream, (((0,), (0,)), ((), ())), preferred_element_type=jnp.float32).astype(jnp.bfloat16)
    grad_weight_in = lax.dot_general(tokens, grad_hidden, (((0,), (0,)), ((), ())), preferred_element_type=jnp.float32).astype(jnp.bfloat16)
    grad_tokens = lax.dot_general(grad_hidden, weight_in, (((1,), (1,)), ((), ())), preferred_element_type=jnp.float32).astype(jnp.bfloat16)
    return (output, grad_tokens, grad_weight_in, grad_weight_out)
```

```python
import math

import jax
import jax.numpy as jnp
from jax import lax
from jax.sharding import PartitionSpec as P


Z, YH, X, YL, C = 4, 2, 4, 2, 2


def permutation(move):
    pairs = []
    for z in range(Z):
        for yh in range(YH):
            for x in range(X):
                for yl in range(YL):
                    for c in range(C):
                        tz, tyh, tx, tyl, tc = move(z, yh, x, yl, c)
                        source = (z * YH + yh) * (X * YL * C) + (x * YL + yl) * C + c
                        target = (tz * YH + tyh) * (X * YL * C) + (tx * YL + tyl) * C + tc
                        pairs.append((source, target))
    return pairs


SWAP_CORE = permutation(lambda z, yh, x, yl, c: (z, yh, x, yl, 1 - c))
SWAP_LO = permutation(lambda z, yh, x, yl, c: (z, yh, x, 1 - yl, c))
SWAP_HI = permutation(lambda z, yh, x, yl, c: (z, 1 - yh, x, yl, c))
X_UP = permutation(lambda z, yh, x, yl, c: (z, yh, (x + 1) % X, yl, c))
X_DOWN = permutation(lambda z, yh, x, yl, c: (z, yh, (x - 1) % X, yl, c))
Z_UP = permutation(lambda z, yh, x, yl, c: ((z + 1) % Z, yh, x, yl, c))
Z_DOWN = permutation(lambda z, yh, x, yl, c: ((z - 1) % Z, yh, x, yl, c))
Z_FAR = permutation(lambda z, yh, x, yl, c: ((z + 2) % Z, yh, x, yl, c))


def send(value, pairs):
    return lax.ppermute(value, ("row", "col"), pairs)


def gelu_value(value):
    return 0.5 * value * (1.0 + jax.scipy.special.erf(value / math.sqrt(2.0)))


def gelu_slope(value):
    normal_part = jnp.exp(-0.5 * value * value) / math.sqrt(2.0 * math.pi)
    return 0.5 * (1.0 + jax.scipy.special.erf(value / math.sqrt(2.0))) + value * normal_part


def dot(left, right, contract):
    return lax.dot_general(
        left, right, ((contract[:1], contract[1:]), ((), ())), preferred_element_type=jnp.float32
    )


def narrow(value):
    return value.astype(jnp.bfloat16)


def ordered(flag, own, other, axis):
    first = jnp.where(flag == 0, own, other)
    second = jnp.where(flag == 0, other, own)
    return jnp.concatenate([first, second], axis=axis)


def halves(value, axis):
    size = value.shape[axis] // 2
    return (
        lax.slice_in_dim(value, 0, size, axis=axis),
        lax.slice_in_dim(value, size, 2 * size, axis=axis),
    )


def mine_and_other(flag, value, axis):
    low, high = halves(value, axis)
    return jnp.where(flag == 0, low, high), jnp.where(flag == 0, high, low)


def body(tokens, weight_in, weight_out, upstream):
    row, col = lax.axis_index("row"), lax.axis_index("col")
    z, yh = row // YH, row % YH
    x, yl, c = col // (YL * C), (col // C) % YL, col % C

    def block(value, index, rows):
        return lax.dynamic_slice_in_dim(value, index % 4 * rows, rows, axis=0)

    def gather_rows(own):
        pair = ordered(yh, own, send(own, SWAP_HI), 0)
        ring = [pair, send(pair, Z_DOWN), send(pair, Z_FAR), send(pair, Z_UP)]
        ring = jnp.concatenate(ring, axis=0)
        rows = pair.shape[0]
        turned = jnp.concatenate([block(ring, x + j - z, rows) for j in range(4)], axis=0)
        return jnp.concatenate([turned, send(turned, SWAP_CORE)], axis=1)

    def reduce_columns(parts):
        low, high = halves(narrow(parts[2]), 0)
        from_down, from_up = send(low, X_UP), send(high, X_DOWN)
        low, high = halves(parts[1], 0)
        up = jnp.concatenate([narrow(low + from_down), narrow(high)], axis=0)
        low, high = halves(parts[3], 0)
        down = jnp.concatenate([narrow(low), narrow(high + from_up)], axis=0)
        total = parts[0] + send(up, X_UP) + send(down, X_DOWN)
        mine, other = mine_and_other(yl, total, 0)
        return mine + send(narrow(other), SWAP_LO)

    def gather_columns(own):
        pair = ordered(yl, own, send(own, SWAP_LO), 0)
        after, before = send(pair, X_DOWN), send(pair, X_UP)
        low, high = send(halves(before, 0)[0], X_UP), send(halves(after, 0)[1], X_DOWN)
        return jnp.concatenate([pair, after, low, high, before], axis=0)

    def reduce_rows(part):
        mine, other = halves(part, 1)
        total = mine + send(other, SWAP_CORE)
        rows = total.shape[0] // 4
        chunks = [block(total, z + k - x, rows) for k in range(4)]
        total = (
            chunks[0]
            + send(narrow(chunks[1]), Z_UP)
            + send(narrow(chunks[2]), Z_FAR)
            + send(narrow(chunks[3]), Z_DOWN)
        )
        mine, other = mine_and_other(yh, total, 0)
        return narrow(mine + send(other, SWAP_HI))

    mine, other = mine_and_other(c, weight_in, 1)
    w_in = jnp.concatenate([mine, send(other, SWAP_CORE)], axis=0)
    mine, other = mine_and_other(c, weight_out, 0)
    w_out = jnp.concatenate([mine, send(other, SWAP_CORE)], axis=1)

    all_tokens = gather_rows(tokens)
    all_upstream = gather_rows(upstream)
    rows = all_tokens.shape[0] // 4

    def chunk(value, j):
        return lax.slice_in_dim(value, j * rows, (j + 1) * rows, axis=0)

    hidden = reduce_columns([dot(chunk(all_tokens, j), w_in, (1, 0)) for j in range(4)])
    grad_act = reduce_columns([dot(chunk(all_upstream, j), w_out, (1, 1)) for j in range(4)])
    act = narrow(gelu_value(hidden))
    grad_hidden = narrow(grad_act * gelu_slope(hidden))

    all_act = gather_columns(act)
    output = reduce_rows(dot(all_act, w_out, (1, 0)))
    part = narrow(dot(all_act, all_upstream, (0, 0)))
    mine, other = halves(part, 1)
    grad_weight_out = ordered(c, mine, send(other, SWAP_CORE), 0)

    all_grad_hidden = gather_columns(grad_hidden)
    grad_tokens = reduce_rows(dot(all_grad_hidden, w_in, (1, 1)))
    part = narrow(dot(all_tokens, all_grad_hidden, (0, 0)))
    mine, other = halves(part, 0)
    grad_weight_in = ordered(c, mine, send(other, SWAP_CORE), 1)
    return (output, grad_tokens, grad_weight_in, grad_weight_out)


def solution(mesh):
    return jax.shard_map(
        body,
        mesh=mesh,
        in_specs=(P("row", "col"), P("col", "row"), P("row", "col"), P("row", "col")),
        out_specs=(P("row", "col"), P("row", "col"), P("col", "row"), P("row", "col")),
        check_vma=False,
    )
```

```python
import math

import jax
import jax.numpy as jnp
from jax import lax
from jax.experimental import pallas as pl
from jax.experimental.pallas import tpu as pltpu
from jax.sharding import PartitionSpec as P


Z, YH, X, YL, C = 4, 2, 4, 2, 2


def permutation(move):
    pairs = []
    for z in range(Z):
        for yh in range(YH):
            for x in range(X):
                for yl in range(YL):
                    for c in range(C):
                        tz, tyh, tx, tyl, tc = move(z, yh, x, yl, c)
                        source = (z * YH + yh) * (X * YL * C) + (x * YL + yl) * C + c
                        target = (tz * YH + tyh) * (X * YL * C) + (tx * YL + tyl) * C + tc
                        pairs.append((source, target))
    return pairs


SWAP_CORE = permutation(lambda z, yh, x, yl, c: (z, yh, x, yl, 1 - c))
SWAP_LO = permutation(lambda z, yh, x, yl, c: (z, yh, x, 1 - yl, c))
X_UP, _, X_DOWN = (
    permutation(lambda z, yh, x, yl, c: (z, yh, (x + k) % X, yl, c)) for k in (1, 2, 3)
)


SWAP_HI = permutation(lambda z, yh, x, yl, c: (z, 1 - yh, x, yl, c))


def row_move(k):
    return permutation(lambda z, yh, x, yl, c: ((z + k) % Z, yh, x, yl, c))


def send(value, pairs):
    return lax.ppermute(value, ("row", "col"), pairs)


def after(value, *earlier):
    return lax.optimization_barrier((value, *earlier))[0]


def gelu_value(value):
    return 0.5 * value * (1.0 + jax.scipy.special.erf(value / math.sqrt(2.0)))


def gelu_slope(value):
    normal_part = jnp.exp(-0.5 * value * value) / math.sqrt(2.0 * math.pi)
    return 0.5 * (1.0 + jax.scipy.special.erf(value / math.sqrt(2.0))) + value * normal_part


def dot(left, right, contract, tiles, dtype=jnp.float32):
    left_at, right_at = contract
    deep, tall, wide = left.shape[left_at], left.shape[1 - left_at], right.shape[1 - right_at]
    rows, columns, strip = tiles

    def kernel(left_ref, right_ref, out_ref):
        @pl.loop(0, rows // strip)
        def _(index):
            span = pl.ds(pl.multiple_of(index * strip, strip), strip)
            part = left_ref[span, :] if left_at else left_ref[:, span]
            out_ref[span, :] = lax.dot_general(
                part,
                right_ref[...],
                (((left_at,), (right_at,)), ((), ())),
                preferred_element_type=jnp.float32,
            ).astype(dtype)

    left_spec = (
        pl.BlockSpec((rows, deep), lambda i, j: (i, 0))
        if left_at
        else pl.BlockSpec((deep, rows), lambda i, j: (0, i))
    )
    right_spec = (
        pl.BlockSpec((columns, deep), lambda i, j: (j, 0))
        if right_at
        else pl.BlockSpec((deep, columns), lambda i, j: (0, j))
    )
    item = jnp.dtype(dtype).itemsize
    return pl.pallas_call(
        kernel,
        grid=(tall // rows, wide // columns),
        in_specs=[left_spec, right_spec],
        out_specs=pl.BlockSpec((rows, columns), lambda i, j: (i, j)),
        out_shape=jax.ShapeDtypeStruct((tall, wide), dtype),
        compiler_params=pltpu.CompilerParams(vmem_limit_bytes=32 << 20),
        cost_estimate=pl.CostEstimate(
            flops=2 * deep * tall * wide,
            transcendentals=0,
            bytes_accessed=2 * deep * (tall + wide) + item * tall * wide,
        ),
    )(left, right)


def narrow(value):
    return value.astype(jnp.bfloat16)


def ordered(flag, own, other, axis):
    first = jnp.where(flag == 0, own, other)
    second = jnp.where(flag == 0, other, own)
    return jnp.concatenate([first, second], axis=axis)


def halves(value, axis):
    size = value.shape[axis] // 2
    return (
        lax.slice_in_dim(value, 0, size, axis=axis),
        lax.slice_in_dim(value, size, 2 * size, axis=axis),
    )


def mine_and_other(flag, value, axis):
    low, high = halves(value, axis)
    return jnp.where(flag == 0, low, high), jnp.where(flag == 0, high, low)


def cut(value, first, last):
    return lax.slice_in_dim(value, first, last, axis=0)


def start_far(far):
    low, high = halves(narrow(far), 0)
    return (send(low, X_UP), send(high, X_DOWN)), low


def start_near(up, down, far):
    rows = far[0].shape[0]
    up = narrow(up + jnp.pad(far[0], ((0, rows), (0, 0))))
    down = narrow(down + jnp.pad(far[1], ((rows, 0), (0, 0))))
    return send(up, X_UP), send(down, X_DOWN), up, down


def finish_columns(own, near):
    total = own + near[0] + near[1]
    return total + send(narrow(total), SWAP_LO)


def gather_far(up, down):
    low, high = halves(down, 0)[0], halves(up, 0)[1]
    return send(low, X_UP), send(high, X_DOWN)


ORDER = (2, 1, 3, 0)


def compute(tokens, weight_in, weight_out, upstream):
    row, col = lax.axis_index("row"), lax.axis_index("col")
    z, x, c = row // YH, col // (YL * C), col % C
    block = 2 * tokens.shape[0]

    def ring(own):
        return [own] + [send(own, row_move(-k)) for k in (1, 2, 3)]

    def turn(blocks):
        stacked = jnp.concatenate(blocks, axis=0)
        return jnp.concatenate(
            [
                lax.dynamic_slice_in_dim(stacked, (x + j - z) % 4 * block, block, axis=0)
                for j in ORDER
            ],
            axis=0,
        )

    def split_rows(far, far_received, near, near_received):
        total = jnp.concatenate([far + far_received, near + near_received], axis=0)
        chunks = []
        for k in range(4):
            place = (z + k - x) % 4
            place = jnp.where(place == 2, 0, jnp.where(place == 0, 3, (place + 1) // 2))
            chunks.append(lax.dynamic_slice_in_dim(total, place * block, block, axis=0))
        return chunks[0], [narrow(v) for v in chunks[1:]]

    def finish_rows(own, parts):
        parts = [send(v, row_move(k)) for k, v in zip((1, 2, 3), parts)]
        mine, other = halves(own + parts[0] + parts[1] + parts[2], 0)
        return mine, send(other, SWAP_HI), other

    tokens = jnp.concatenate([tokens, send(tokens, SWAP_HI)], axis=0)
    upstream = jnp.concatenate([upstream, send(upstream, SWAP_HI)], axis=0)
    tokens_ring = ring(tokens)
    in_mine, in_other = mine_and_other(c, weight_in, 1)
    in_received = send(in_other, SWAP_CORE)
    out_mine, out_other = mine_and_other(c, weight_out, 0)
    upstream_ring = ring(upstream)
    turned = turn(tokens_ring)
    all_tokens = jnp.concatenate([turned, send(turned, SWAP_CORE)], axis=1)
    w_in = jnp.concatenate([in_mine, in_received], axis=0)
    out_received = send(out_other, SWAP_CORE)
    w_out = jnp.concatenate([out_mine, out_received], axis=1)

    h_far, sent = start_far(dot(cut(all_tokens, 0, block), w_in, (1, 0), (256, 512, 256)))
    h_part = dot(after(cut(all_tokens, block, 4 * block), sent), w_in, (1, 0), (768, 512, 256))
    h_near = start_near(cut(h_part, 0, block), cut(h_part, block, 2 * block), h_far)
    upstream_ring = lax.optimization_barrier((*upstream_ring, *h_near[2:]))[:4]
    turned = turn(upstream_ring)
    all_upstream = jnp.concatenate([turned, send(turned, SWAP_CORE)], axis=1)
    g_part = dot(all_upstream, w_out, (1, 1), (1024, 512, 256))
    g_far, sent = start_far(cut(g_part, 0, block))
    hidden = finish_columns(after(cut(h_part, 2 * block, 3 * block), sent), h_near)
    g_near = start_near(cut(g_part, block, 2 * block), cut(g_part, 2 * block, 3 * block), g_far)

    act, slope = lax.optimization_barrier((narrow(gelu_value(hidden)), gelu_slope(hidden)))
    a_up, a_down = send(act, X_DOWN), send(act, X_UP)
    grad_act = finish_columns(after(cut(g_part, 3 * block, 4 * block), act), g_near)
    a_low, a_high = gather_far(a_up, a_down)
    grad_hidden = narrow(grad_act * slope)
    b_up, b_down = send(grad_hidden, X_DOWN), send(grad_hidden, X_UP)

    act_near = jnp.concatenate([after(a_up, grad_hidden), a_down, act], axis=0)
    mine, other = halves(dot(act_near, w_out, (1, 0), (768, 512, 256)), 1)
    near = mine, send(other, SWAP_CORE)
    act_far = jnp.concatenate([after(a_low, other), a_high], axis=0)
    mine, other = halves(dot(act_far, w_out, (1, 0), (256, 512, 256)), 1)
    far = mine, send(other, SWAP_CORE)
    all_act = jnp.concatenate([after(act_far, other), act_near], axis=0)
    part = dot(all_act, all_upstream, (0, 0), (512, 1024, 256), jnp.bfloat16)
    out_part, other = halves(part, 1)
    out_received = send(other, SWAP_CORE)
    own, parts = split_rows(after(far[0], other), far[1], *near)
    o_mine, o_received, _ = finish_rows(own, parts)
    b_low, b_high = gather_far(after(b_up, *parts), b_down)

    grad_near = jnp.concatenate([b_up, b_down, grad_hidden], axis=0)
    mine, other = halves(dot(grad_near, w_in, (1, 1), (768, 512, 256)), 1)
    near = mine, send(other, SWAP_CORE)
    grad_far = jnp.concatenate([after(b_low, other), b_high], axis=0)
    mine, other = halves(dot(grad_far, w_in, (1, 1), (256, 512, 256)), 1)
    far = mine, send(other, SWAP_CORE)
    own, parts = split_rows(*far, *near)
    all_grad = jnp.concatenate([after(grad_far, own, *parts), grad_near], axis=0)
    part = dot(all_tokens, all_grad, (0, 0), (512, 1024, 256), jnp.bfloat16)
    in_part, other = halves(part, 0)
    in_received = send(other, SWAP_CORE)
    out_received = after(out_received, part)
    grad_weight_out = ordered(c, out_part, out_received, 0)
    r_mine, r_received, r_other = finish_rows(after(own, part), parts)

    output = narrow(o_mine + o_received)
    in_received = after(in_received, r_other)
    grad_weight_in = ordered(c, in_part, in_received, 1)
    grad_tokens = narrow(r_mine + r_received)
    return (output, grad_tokens, grad_weight_in, grad_weight_out)


def solution(mesh):
    return jax.shard_map(
        compute,
        mesh=mesh,
        in_specs=(P("row", "col"), P("col", "row"), P("row", "col"), P("row", "col")),
        out_specs=(P("row", "col"), P("row", "col"), P("col", "row"), P("row", "col")),
        check_vma=False,
    )
```

```python
import math

import jax
import jax.numpy as jnp
from jax import lax
from jax.experimental import pallas as pl
from jax.experimental.pallas import tpu as pltpu
from jax.sharding import PartitionSpec as P


Z, YH, X, YL, C = 4, 2, 4, 2, 2


def permutation(move):
    pairs = []
    for z in range(Z):
        for yh in range(YH):
            for x in range(X):
                for yl in range(YL):
                    for c in range(C):
                        tz, tyh, tx, tyl, tc = move(z, yh, x, yl, c)
                        source = (z * YH + yh) * (X * YL * C) + (x * YL + yl) * C + c
                        target = (tz * YH + tyh) * (X * YL * C) + (tx * YL + tyl) * C + tc
                        pairs.append((source, target))
    return pairs


SWAP_CORE = permutation(lambda z, yh, x, yl, c: (z, yh, x, yl, 1 - c))
SWAP_LO = permutation(lambda z, yh, x, yl, c: (z, yh, x, 1 - yl, c))
X_UP, _, X_DOWN = (
    permutation(lambda z, yh, x, yl, c: (z, yh, (x + k) % X, yl, c)) for k in (1, 2, 3)
)


SWAP_HI = permutation(lambda z, yh, x, yl, c: (z, 1 - yh, x, yl, c))


def row_move(k):
    return permutation(lambda z, yh, x, yl, c: ((z + k) % Z, yh, x, yl, c))


def send(value, pairs):
    return lax.ppermute(value, ("row", "col"), pairs)


def after(value, *earlier):
    return lax.optimization_barrier((value, *earlier))[0]


def gelu_value(value):
    return 0.5 * value * (1.0 + jax.scipy.special.erf(value / math.sqrt(2.0)))


def gelu_slope(value):
    normal_part = jnp.exp(-0.5 * value * value) / math.sqrt(2.0 * math.pi)
    return 0.5 * (1.0 + jax.scipy.special.erf(value / math.sqrt(2.0))) + value * normal_part


def dot(left, right, contract, tiles, dtype=jnp.float32):
    left_at, right_at = contract
    deep, tall, wide = left.shape[left_at], left.shape[1 - left_at], right.shape[1 - right_at]
    rows, columns, strip = tiles

    def kernel(left_ref, right_ref, out_ref):
        @pl.loop(0, rows // strip)
        def _(index):
            span = pl.ds(pl.multiple_of(index * strip, strip), strip)
            part = left_ref[span, :] if left_at else left_ref[:, span]
            out_ref[span, :] = lax.dot_general(
                part,
                right_ref[...],
                (((left_at,), (right_at,)), ((), ())),
                preferred_element_type=jnp.float32,
            ).astype(dtype)

    left_spec = (
        pl.BlockSpec((rows, deep), lambda i, j: (i, 0))
        if left_at
        else pl.BlockSpec((deep, rows), lambda i, j: (0, i))
    )
    right_spec = (
        pl.BlockSpec((columns, deep), lambda i, j: (j, 0))
        if right_at
        else pl.BlockSpec((deep, columns), lambda i, j: (0, j))
    )
    item = jnp.dtype(dtype).itemsize
    return pl.pallas_call(
        kernel,
        grid=(tall // rows, wide // columns),
        in_specs=[left_spec, right_spec],
        out_specs=pl.BlockSpec((rows, columns), lambda i, j: (i, j)),
        out_shape=jax.ShapeDtypeStruct((tall, wide), dtype),
        compiler_params=pltpu.CompilerParams(vmem_limit_bytes=16 << 20),
        cost_estimate=pl.CostEstimate(
            flops=2 * deep * tall * wide,
            transcendentals=0,
            bytes_accessed=2 * deep * (tall + wide) + item * tall * wide,
        ),
    )(left, right)


def narrow(value):
    return value.astype(jnp.bfloat16)


def ordered(flag, own, other, axis):
    first = jnp.where(flag == 0, own, other)
    second = jnp.where(flag == 0, other, own)
    return jnp.concatenate([first, second], axis=axis)


def halves(value, axis):
    size = value.shape[axis] // 2
    return (
        lax.slice_in_dim(value, 0, size, axis=axis),
        lax.slice_in_dim(value, size, 2 * size, axis=axis),
    )


def mine_and_other(flag, value, axis):
    low, high = halves(value, axis)
    return jnp.where(flag == 0, low, high), jnp.where(flag == 0, high, low)


def cut(value, first, last):
    return lax.slice_in_dim(value, first, last, axis=0)


def start_far(far):
    low, high = halves(narrow(far), 0)
    return (send(low, X_UP), send(high, X_DOWN)), low


def start_near(up, down, far):
    up, down = halves(up, 0), halves(down, 0)
    early = narrow(up[1]), narrow(down[0])
    late = narrow(up[0] + far[0]), narrow(down[1] + far[1])
    parts = [send(early[0], X_UP), send(early[1], X_DOWN)]
    parts += [send(late[0], X_UP), send(late[1], X_DOWN)]
    return parts, early, late


def finish_columns(own, parts):
    low, high = halves(own, 0)
    total = jnp.concatenate([low + parts[2] + parts[1], high + parts[0] + parts[3]], axis=0)
    return total + send(narrow(total), SWAP_LO)


def gather_far(up, down):
    low, high = halves(down, 0)[0], halves(up, 0)[1]
    return send(low, X_UP), send(high, X_DOWN)


ORDER = (2, 1, 3, 0)


def compute(tokens, weight_in, weight_out, upstream):
    row, col = lax.axis_index("row"), lax.axis_index("col")
    z, x, c = row // YH, col // (YL * C), col % C
    block = 2 * tokens.shape[0]

    def ring(own):
        return [own] + [send(own, row_move(-k)) for k in (1, 2, 3)]

    def turn(blocks):
        stacked = jnp.concatenate(blocks, axis=0)
        return jnp.concatenate(
            [
                lax.dynamic_slice_in_dim(stacked, (x + j - z) % 4 * block, block, axis=0)
                for j in ORDER
            ],
            axis=0,
        )

    def split_rows(far, far_received, near, near_received):
        total = jnp.concatenate([far + far_received, near + near_received], axis=0)
        total = lax.optimization_barrier(total)
        chunks = []
        for k in range(4):
            place = (z + k - x) % 4
            place = jnp.where(place == 2, 0, jnp.where(place == 0, 3, (place + 1) // 2))
            chunks.append(lax.dynamic_slice_in_dim(total, place * block, block, axis=0))
        return chunks[0], [narrow(v) for v in chunks[1:]]

    def finish_rows(own, parts):
        parts = [send(v, row_move(k)) for k, v in zip((1, 2, 3), parts)]
        mine, other = halves(own + parts[0] + parts[1] + parts[2], 0)
        return mine, send(other, SWAP_HI), other

    received = send(tokens, SWAP_HI)
    tokens_ring = [v for own, other in zip(ring(tokens), ring(received)) for v in (own, other)]
    upstream = jnp.concatenate([upstream, send(upstream, SWAP_HI)], axis=0)
    in_mine, in_other = mine_and_other(c, weight_in, 1)
    in_received = send(in_other, SWAP_CORE)
    out_mine, out_other = mine_and_other(c, weight_out, 0)
    upstream_ring = ring(upstream)
    turned = turn(tokens_ring)
    all_tokens = jnp.concatenate([turned, send(turned, SWAP_CORE)], axis=1)
    w_in = jnp.concatenate([in_mine, in_received], axis=0)
    out_received = send(out_other, SWAP_CORE)
    w_out = jnp.concatenate([out_mine, out_received], axis=1)

    h_far, sent = start_far(dot(cut(all_tokens, 0, block), w_in, (1, 0), (256, 512, 256)))
    h_part = dot(after(cut(all_tokens, block, 4 * block), sent), w_in, (1, 0), (768, 512, 256))
    h_parts, _, late = start_near(cut(h_part, 0, block), cut(h_part, block, 2 * block), h_far)
    upstream_ring = lax.optimization_barrier((*upstream_ring, *late))[:4]
    turned = turn(upstream_ring)
    all_upstream = jnp.concatenate([turned, send(turned, SWAP_CORE)], axis=1)
    g_part = dot(all_upstream, w_out, (1, 1), (1024, 512, 256))
    g_far, sent = start_far(cut(g_part, 0, block))
    g_parts, early, _ = start_near(cut(g_part, block, 2 * block), cut(g_part, 2 * block, 3 * block), g_far)
    h_parts = lax.optimization_barrier((*h_parts, sent, *early))[:4]
    hidden = finish_columns(cut(h_part, 2 * block, 3 * block), h_parts)

    act, slope = lax.optimization_barrier((narrow(gelu_value(hidden)), gelu_slope(hidden)))
    a_up, a_down = send(act, X_DOWN), send(act, X_UP)
    g_parts = lax.optimization_barrier((*g_parts, act))[:4]
    grad_act = finish_columns(cut(g_part, 3 * block, 4 * block), g_parts)
    a_low, a_high = gather_far(a_up, a_down)
    grad_hidden = narrow(grad_act * slope)
    b_up, b_down = send(grad_hidden, X_DOWN), send(grad_hidden, X_UP)

    act_near = jnp.concatenate([after(a_up, grad_hidden), a_down, act], axis=0)
    mine, other = halves(dot(act_near, w_out, (1, 0), (768, 512, 256)), 1)
    near = mine, send(other, SWAP_CORE)
    act_far = jnp.concatenate([after(a_low, other), a_high], axis=0)
    mine, other = halves(dot(act_far, w_out, (1, 0), (256, 512, 256)), 1)
    far = mine, send(other, SWAP_CORE)
    all_act = jnp.concatenate([after(act_far, other), act_near], axis=0)
    part = dot(all_act, all_upstream, (0, 0), (512, 1024, 256), jnp.bfloat16)
    out_part, other = halves(part, 1)
    out_received = send(other, SWAP_CORE)
    own, parts = split_rows(after(far[0], other), far[1], *near)
    o_mine, o_received, _ = finish_rows(own, parts)
    b_low, b_high = gather_far(after(b_up, *parts), b_down)

    grad_near = jnp.concatenate([b_up, b_down, grad_hidden], axis=0)
    mine, other = halves(dot(grad_near, w_in, (1, 1), (768, 512, 256)), 1)
    near = mine, send(other, SWAP_CORE)
    grad_far = jnp.concatenate([after(b_low, other), b_high], axis=0)
    mine, other = halves(dot(grad_far, w_in, (1, 1), (256, 512, 256)), 1)
    far = mine, send(other, SWAP_CORE)
    own, parts = split_rows(*far, *near)
    all_grad = jnp.concatenate([after(grad_far, own, *parts), grad_near], axis=0)
    part = dot(all_tokens, all_grad, (0, 0), (512, 1024, 256), jnp.bfloat16)
    in_part, other = halves(part, 0)
    in_received = send(other, SWAP_CORE)
    r_mine, r_received, r_other = finish_rows(after(own, part), parts)

    output = narrow(o_mine + o_received)
    out_received, in_received = lax.optimization_barrier((out_received, in_received, r_other))[:2]
    grad_weight_out = ordered(c, out_part, out_received, 0)
    grad_weight_in = ordered(c, in_part, in_received, 1)
    grad_tokens = narrow(r_mine + r_received)
    return (output, grad_tokens, grad_weight_in, grad_weight_out)


def solution(mesh):
    return jax.shard_map(
        compute,
        mesh=mesh,
        in_specs=(P("row", "col"), P("col", "row"), P("row", "col"), P("row", "col")),
        out_specs=(P("row", "col"), P("row", "col"), P("col", "row"), P("row", "col")),
        check_vma=False,
    )
```

```python
import math

import jax
import jax.numpy as jnp
from jax import lax
from jax.experimental import pallas as pl
from jax.experimental.pallas import tpu as pltpu
from jax.sharding import PartitionSpec as P


Z, YH, X, YL, C = 4, 2, 4, 2, 2


def permutation(move):
    pairs = []
    for z in range(Z):
        for yh in range(YH):
            for x in range(X):
                for yl in range(YL):
                    for c in range(C):
                        tz, tyh, tx, tyl, tc = move(z, yh, x, yl, c)
                        source = (z * YH + yh) * (X * YL * C) + (x * YL + yl) * C + c
                        target = (tz * YH + tyh) * (X * YL * C) + (tx * YL + tyl) * C + tc
                        pairs.append((source, target))
    return pairs


SWAP_CORE = permutation(lambda z, yh, x, yl, c: (z, yh, x, yl, 1 - c))
SWAP_LO = permutation(lambda z, yh, x, yl, c: (z, yh, x, 1 - yl, c))
X_UP, _, X_DOWN = (
    permutation(lambda z, yh, x, yl, c: (z, yh, (x + k) % X, yl, c)) for k in (1, 2, 3)
)


SWAP_HI = permutation(lambda z, yh, x, yl, c: (z, 1 - yh, x, yl, c))


def row_move(k):
    return permutation(lambda z, yh, x, yl, c: ((z + k) % Z, yh, x, yl, c))


def send(value, pairs):
    return lax.ppermute(value, ("row", "col"), pairs)


def after(value, *earlier):
    return lax.optimization_barrier((value, *earlier))[0]


def gelu_value(value):
    return 0.5 * value * (1.0 + jax.scipy.special.erf(value / math.sqrt(2.0)))


def gelu_slope(value):
    normal_part = jnp.exp(-0.5 * value * value) / math.sqrt(2.0 * math.pi)
    return 0.5 * (1.0 + jax.scipy.special.erf(value / math.sqrt(2.0))) + value * normal_part


def dot(left, right, contract, tiles, dtype=jnp.float32):
    left_at, right_at = contract
    deep, tall, wide = left.shape[left_at], left.shape[1 - left_at], right.shape[1 - right_at]
    rows, columns, strip = tiles

    def kernel(left_ref, right_ref, out_ref):
        @pl.loop(0, rows // strip)
        def _(index):
            span = pl.ds(pl.multiple_of(index * strip, strip), strip)
            part = left_ref[span, :] if left_at else left_ref[:, span]
            out_ref[span, :] = lax.dot_general(
                part,
                right_ref[...],
                (((left_at,), (right_at,)), ((), ())),
                preferred_element_type=jnp.float32,
            ).astype(dtype)

    left_spec = (
        pl.BlockSpec((rows, deep), lambda i, j: (i, 0))
        if left_at
        else pl.BlockSpec((deep, rows), lambda i, j: (0, i))
    )
    right_spec = (
        pl.BlockSpec((columns, deep), lambda i, j: (j, 0))
        if right_at
        else pl.BlockSpec((deep, columns), lambda i, j: (0, j))
    )
    item = jnp.dtype(dtype).itemsize
    return pl.pallas_call(
        kernel,
        grid=(tall // rows, wide // columns),
        in_specs=[left_spec, right_spec],
        out_specs=pl.BlockSpec((rows, columns), lambda i, j: (i, j)),
        out_shape=jax.ShapeDtypeStruct((tall, wide), dtype),
        compiler_params=pltpu.CompilerParams(vmem_limit_bytes=12 << 20),
        cost_estimate=pl.CostEstimate(
            flops=2 * deep * tall * wide,
            transcendentals=0,
            bytes_accessed=2 * deep * (tall + wide) + item * tall * wide,
        ),
    )(left, right)


def joined_dot(left, right, tiles):
    tall, wide = left[0].shape[1], right[0].shape[1]
    rows, columns = tiles

    def kernel(*refs):
        parts = [ref[...] for ref in refs[:-1]]
        left_part = jnp.concatenate(parts[: len(left)], axis=0)
        right_part = jnp.concatenate(parts[len(left) :], axis=0)
        refs[-1][...] = lax.dot_general(
            left_part, right_part, (((0,), (0,)), ((), ())), preferred_element_type=jnp.float32
        ).astype(jnp.bfloat16)

    return pl.pallas_call(
        kernel,
        grid=(wide // columns, tall // rows),
        in_specs=[pl.BlockSpec((v.shape[0], rows), lambda j, i: (0, i)) for v in left]
        + [pl.BlockSpec((v.shape[0], columns), lambda j, i: (0, j)) for v in right],
        out_specs=pl.BlockSpec((rows, columns), lambda j, i: (i, j)),
        out_shape=jax.ShapeDtypeStruct((tall, wide), jnp.bfloat16),
        compiler_params=pltpu.CompilerParams(vmem_limit_bytes=12 << 20),
        cost_estimate=pl.CostEstimate(
            flops=2048 * tall * wide, transcendentals=0, bytes_accessed=2048 * (tall + wide)
        ),
    )(*left, *right)


def narrow(value):
    return value.astype(jnp.bfloat16)


def ordered(flag, own, other, axis):
    first = jnp.where(flag == 0, own, other)
    second = jnp.where(flag == 0, other, own)
    return jnp.concatenate([first, second], axis=axis)


def halves(value, axis):
    size = value.shape[axis] // 2
    return (
        lax.slice_in_dim(value, 0, size, axis=axis),
        lax.slice_in_dim(value, size, 2 * size, axis=axis),
    )


def mine_and_other(flag, value, axis):
    low, high = halves(value, axis)
    return jnp.where(flag == 0, low, high), jnp.where(flag == 0, high, low)


def cut(value, first, last):
    return lax.slice_in_dim(value, first, last, axis=0)


def start_far(far):
    low, high = halves(narrow(far), 0)
    return (send(low, X_UP), send(high, X_DOWN)), low


def start_near(up, down, far):
    up, down = halves(up, 0), halves(down, 0)
    early = narrow(up[1]), narrow(down[0])
    late = narrow(up[0] + far[0]), narrow(down[1] + far[1])
    parts = [send(early[0], X_UP), send(early[1], X_DOWN)]
    parts += [send(late[0], X_UP), send(late[1], X_DOWN)]
    return parts, early, late


def finish_columns(own, parts):
    low, high = halves(own, 0)
    total = jnp.concatenate([low + parts[2] + parts[1], high + parts[0] + parts[3]], axis=0)
    return total + send(narrow(total), SWAP_LO)


def gather_far(up, down):
    low, high = halves(down, 0)[0], halves(up, 0)[1]
    return send(low, X_UP), send(high, X_DOWN)


ORDER = (2, 1, 3, 0)


def compute(tokens, weight_in, weight_out, upstream):
    row, col = lax.axis_index("row"), lax.axis_index("col")
    z, x, c = row // YH, col // (YL * C), col % C
    block = 2 * tokens.shape[0]

    def ring(own):
        return [own] + [send(own, row_move(-k)) for k in (1, 2, 3)]

    def turn(blocks):
        stacked = jnp.concatenate(blocks, axis=0)
        return jnp.concatenate(
            [
                lax.dynamic_slice_in_dim(stacked, (x + j - z) % 4 * block, block, axis=0)
                for j in ORDER
            ],
            axis=0,
        )

    def split_rows(far, far_received, near, near_received):
        total = jnp.concatenate([far + far_received, near + near_received], axis=0)
        total = lax.optimization_barrier(total)
        chunks = []
        for k in range(4):
            place = (z + k - x) % 4
            place = jnp.where(place == 2, 0, jnp.where(place == 0, 3, (place + 1) // 2))
            chunks.append(lax.dynamic_slice_in_dim(total, place * block, block, axis=0))
        return chunks[0], [narrow(v) for v in chunks[1:]]

    def finish_rows(own, parts):
        parts = [send(v, row_move(k + 1)) for k, v in enumerate(parts)]
        mine, other = halves(own + parts[0] + parts[1] + parts[2], 0)
        return mine, send(other, SWAP_HI), other

    received = send(tokens, SWAP_HI)
    tokens_ring = [v for own, other in zip(ring(tokens), ring(received)) for v in (own, other)]
    upstream = jnp.concatenate([upstream, send(upstream, SWAP_HI)], axis=0)
    in_mine, in_other = mine_and_other(c, weight_in, 1)
    in_received = send(in_other, SWAP_CORE)
    out_mine, out_other = mine_and_other(c, weight_out, 0)
    upstream_ring = ring(upstream)
    turned = turn(tokens_ring)
    all_tokens = jnp.concatenate([turned, send(turned, SWAP_CORE)], axis=1)
    w_in = jnp.concatenate([in_mine, in_received], axis=0)
    out_received = send(out_other, SWAP_CORE)
    w_out = jnp.concatenate([out_mine, out_received], axis=1)

    h_far, sent = start_far(dot(cut(all_tokens, 0, block), w_in, (1, 0), (256, 512, 256)))
    h_part = dot(after(cut(all_tokens, block, 4 * block), sent), w_in, (1, 0), (768, 512, 256))
    h_parts, _, late = start_near(cut(h_part, 0, block), cut(h_part, block, 2 * block), h_far)
    upstream_ring = lax.optimization_barrier((*upstream_ring, *late))[:4]
    turned = turn(upstream_ring)
    all_upstream = jnp.concatenate([turned, send(turned, SWAP_CORE)], axis=1)
    g_part = dot(all_upstream, w_out, (1, 1), (1024, 512, 256))
    g_far, sent = start_far(cut(g_part, 0, block))
    g_parts, early, _ = start_near(cut(g_part, block, 2 * block), cut(g_part, 2 * block, 3 * block), g_far)
    h_parts = lax.optimization_barrier((*h_parts, sent, *early))[:4]
    hidden = finish_columns(cut(h_part, 2 * block, 3 * block), h_parts)

    act, slope = lax.optimization_barrier((narrow(gelu_value(hidden)), gelu_slope(hidden)))
    a_up, a_down = send(act, X_DOWN), send(act, X_UP)
    g_parts = lax.optimization_barrier((*g_parts, act))[:4]
    grad_act = finish_columns(cut(g_part, 3 * block, 4 * block), g_parts)
    a_low, a_high = gather_far(a_up, a_down)
    grad_hidden = narrow(grad_act * slope)
    b_up, b_down = send(grad_hidden, X_DOWN), send(grad_hidden, X_UP)

    act_near = jnp.concatenate([after(a_up, grad_hidden), a_down, act], axis=0)
    mine, other = halves(dot(act_near, w_out, (1, 0), (768, 256, 256)), 1)
    near = mine, send(other, SWAP_CORE)
    act_far = jnp.concatenate([after(a_low, other), a_high], axis=0)
    mine, other = halves(dot(act_far, w_out, (1, 0), (256, 512, 256)), 1)
    far = mine, send(other, SWAP_CORE)
    all_act = jnp.concatenate([after(act_far, other), act_near], axis=0)
    part = dot(all_act, all_upstream, (0, 0), (512, 1024, 256), jnp.bfloat16)
    out_part, other = halves(part, 1)
    out_received = send(other, SWAP_CORE)
    own, parts = split_rows(after(far[0], other), far[1], *near)
    o_mine, o_received, _ = finish_rows(own, parts)
    b_low, b_high = gather_far(after(b_up, *parts), b_down)

    grad_near = jnp.concatenate([b_up, b_down, grad_hidden], axis=0)
    mine, other = halves(dot(grad_near, w_in, (1, 1), (768, 256, 256)), 1)
    near = mine, send(other, SWAP_CORE)
    grad_far = jnp.concatenate([after(b_low, other), b_high], axis=0)
    mine, other = halves(dot(grad_far, w_in, (1, 1), (256, 512, 256)), 1)
    far = mine, send(other, SWAP_CORE)
    own, parts = split_rows(*far, *near)
    part = joined_dot((all_tokens,), (after(grad_far, own, *parts), grad_near), (512, 1024))
    in_part, other = halves(part, 0)
    in_received = send(other, SWAP_CORE)
    r_mine, r_received, r_other = finish_rows(after(own, part), parts)

    output = narrow(o_mine + o_received)
    out_received, in_received = lax.optimization_barrier((out_received, in_received, r_other))[:2]
    grad_weight_out = ordered(c, out_part, out_received, 0)
    grad_weight_in = ordered(c, in_part, in_received, 1)
    grad_tokens = narrow(r_mine + r_received)
    return (output, grad_tokens, grad_weight_in, grad_weight_out)


def solution(mesh):
    return jax.shard_map(
        compute,
        mesh=mesh,
        in_specs=(P("row", "col"), P("col", "row"), P("row", "col"), P("row", "col")),
        out_specs=(P("row", "col"), P("row", "col"), P("col", "row"), P("row", "col")),
        check_vma=False,
    )
```
